32 devices in a mesh: gx: 8 (over z, y), gy: 4 (over x, core).
Axes of the slice: x: 2, y: 2, z: 4, core: 2. Of those that a mesh axis runs over, the one named last changes fastest.
Arguments:
- block_input: bfloat16 [512, 8, 1024], P('gx', None, 'gy'), may hold values from -23 to 23
- attn_gain: float32 [1024], P('gy'), may hold values from 0.1 to 1.9
- qkv_weight: bfloat16 [1024, 3072], P('gy', 'gx'), may hold values from -1 to 1
- attn_weight: bfloat16 [1024, 1024], P('gy', 'gx'), may hold values from -1.5 to 1.5
- mlp_gain: float32 [1024], P('gy'), may hold values from 0.1 to 1.9
- inner_weight: bfloat16 [1024, 5248], P('gy', 'gx'), may hold values from -0.1875 to 0.1875
- outer_weight: bfloat16 [2624, 1024], P('gy', 'gx'), may hold values from -0.125 to 0.125
- output_grad: bfloat16 [512, 8, 1024], P('gx', None, 'gy'), may hold values from -6 to 6
Outputs:
- block_output: float32 [512, 8, 1024], P('gx', None, 'gy')
- input_grad: float32 [512, 8, 1024], P('gx', None, 'gy')
- attn_gain_grad: float32 [1024], P('gy')
- qkv_grad: float32 [1024, 3072], P('gy', 'gx')
- attn_weight_grad: float32 [1024, 1024], P('gy', 'gx')
- mlp_gain_grad: float32 [1024], P('gy')
- inner_grad: float32 [1024, 5248], P('gy', 'gx')
- outer_grad: float32 [2624, 1024], P('gy', 'gx')
The draws below stay inside these ranges and needn't reach their ends.
All inputs are finite; a program needn't handle non-finite values.
Results may differ from the reference program's by a relative error of at most 0.014.
Values may be sent and summed in bfloat16 or wider, within the bound.
No kernel may reach another device: no remote copies, remote signals or barrier semaphores. Data moves between devices by JAX's collectives and lax.ppermute only.
A program may use at most 128 MiB of HBM per device.

```python
import math
import jax
import jax.numpy as jnp
from jax import lax

D = 1024
HEADS = 16
HD = 64
FF = 2624
LEN = 512
WINDOW = 128
SEQS = 8


def draw_block_input(key, part):
    key_one, key_two, key_three = jax.random.split(key, 3)
    column = jnp.exp(jnp.linspace(math.log(0.6), math.log(1.8), D)) * jax.random.uniform(key_two, (D,), minval=0.8, maxval=1.25)
    row_scale = jnp.exp(jax.random.uniform(key_three, (LEN, SEQS, 1), minval=-0.9, maxval=0.9))
    values = jax.random.truncated_normal(key_one, -4.0, 4.0, (LEN, SEQS, D)) * row_scale * column
    return values.astype(jnp.bfloat16)


def draw_qkv_weight(key, part):
    key_one = jax.random.fold_in(key, 0)
    values = jax.random.truncated_normal(key_one, -4.0, 4.0, (D, 3 * D)) / math.sqrt(D)
    return values.astype(jnp.bfloat16)


def strengthened(drawn, own_key, source, target, parts, factor):
    def block_of(dim):
        return (jnp.arange(drawn.shape[dim]) // (drawn.shape[dim] // parts)).reshape((-1,) + (1,) * (drawn.ndim - 1 - dim))

    one_side = jax.random.permutation(own_key, parts)[block_of(target)]
    far = (block_of(target) + parts // 2) % parts
    return jnp.where((block_of(source) == one_side) | (block_of(source) == far), factor * drawn, drawn)


def block_scale(key, extent, cuts, least, high):
    level = 1.0
    for axis_at, shards_of in cuts:
        heights = jax.random.uniform(jax.random.fold_in(jax.random.fold_in(key, 6), axis_at), (shards_of,), jnp.float32, least / len(cuts), high / len(cuts))
        level = level * jnp.repeat(jnp.exp(heights), extent[axis_at] // shards_of).reshape((-1,) + (1,) * (len(extent) - 1 - axis_at))
    return level


def bell_draw(own_key, extent, deviation, limit, pieces=(), kind=jnp.bfloat16):
    drawn = deviation * jax.random.normal(own_key, extent, jnp.float32)
    if pieces:
        drawn = drawn * block_scale(own_key, extent, pieces, -0.22, 0.18)
    return jnp.clip(drawn, -limit, limit).astype(kind)


def noise_with(stream_key, extent, scale, limit, cuts, heavy, kind=jnp.bfloat16):
    array = scale * jax.random.normal(stream_key, extent, jnp.float32)
    if cuts:
        array = array * block_scale(stream_key, extent, cuts, -0.22, 0.18)
    return jnp.clip(strengthened(array, jax.random.fold_in(stream_key, 3), *heavy), -limit, limit).astype(kind)


def setup_inputs(seed: int = 0) -> dict:
    seeds = jax.random.split(jax.random.key(seed), 9)
    block_input = draw_block_input(jax.random.fold_in(seeds[8], 71), 0)
    attn_gain = jnp.clip(1.0 + 0.18 * jax.random.normal(seeds[1], (D,), jnp.float32), 0.1, 1.9)
    qkv_weight = draw_qkv_weight(jax.random.fold_in(seeds[8], 71), 0)
    attn_weight = bell_draw(seeds[3], (D, D), (D // 64) ** -0.5, 1.5, ((0, 4), (1, 8)))
    mlp_gain = jnp.clip(1.0 + 0.18 * jax.random.normal(seeds[4], (D,), jnp.float32), 0.1, 1.9)
    inner_weight = bell_draw(seeds[5], (D, 2 * FF), D ** -0.5, 0.1875, ((0, 4), (1, 8)))
    outer_weight = bell_draw(seeds[6], (FF, D), FF ** -0.5, 0.125, ((0, 4), (1, 8)))
    output_grad = noise_with(seeds[7], (LEN, SEQS, D), 1.0, 6.0, ((0, 8), (2, 4)), (0, 2, 8, 2.0))
    return dict(block_input=block_input, attn_gain=attn_gain, qkv_weight=qkv_weight, attn_weight=attn_weight, mlp_gain=mlp_gain, inner_weight=inner_weight, outer_weight=outer_weight, output_grad=output_grad)


epsilon = 1e-05
rope_base = 10000.0

def rope_tables(length, size):
    half_size = size // 2
    frequency = rope_base ** (-(2.0 * jnp.arange(half_size, dtype=jnp.float32)) / size)
    angles = jnp.arange(length, dtype=jnp.float32)[:, None] * frequency[None, :]
    cosine_table = jnp.concatenate([jnp.cos(angles), jnp.cos(angles)], axis=1)
    sine_table = jnp.concatenate([jnp.sin(angles), jnp.sin(angles)], axis=1)
    return (cosine_table[:, None, :], sine_table[:, None, :])

def rotate(values, cosine_table, sine_table):
    half_size = values.shape[-1] // 2
    turned = jnp.concatenate([-values[..., half_size:], values[..., :half_size]], axis=-1)
    return values * cosine_table + turned * sine_table

def rotate_back(grads, cosine_table, sine_table):
    half_size = grads.shape[-1] // 2
    scaled = grads * sine_table
    turned = jnp.concatenate([scaled[..., half_size:], -scaled[..., :half_size]], axis=-1)
    return grads * cosine_table + turned

def norm_stats(values):
    center = lax.optimization_barrier(jnp.mean(values, axis=-1, keepdims=True))
    spread = lax.optimization_barrier(jnp.mean((values - center) ** 2, axis=-1, keepdims=True))
    rescale = lax.rsqrt(spread + epsilon)
    return ((values - center) * rescale, rescale)

def norm_back(grads, normed, rescale, gain):
    scaled = grads * gain
    first_mean = lax.optimization_barrier(jnp.mean(scaled, axis=-1, keepdims=True))
    second_mean = lax.optimization_barrier(jnp.mean(scaled * normed, axis=-1, keepdims=True))
    return rescale * (scaled - first_mean - normed * second_mean)

def gelu_parts(gate_part):
    cumulative = 0.5 * (1.0 + lax.erf(gate_part * 0.7071067811865476))
    density = jnp.exp(-0.5 * gate_part * gate_part) * 0.3989422804014327
    return (gate_part * cumulative, cumulative + gate_part * density)

def masked_scores(queries, key_rows, in_band):
    factor = 1.0 / math.sqrt(queries.shape[-1])
    scores = jnp.einsum('qhd,khd->hqk', queries.astype(jnp.float32), key_rows.astype(jnp.float32)) * factor
    return jnp.where(in_band[None], scores, -jnp.inf)

def attend(queries, key_rows, value_rows, in_band):
    scores = masked_scores(queries, key_rows, in_band)
    row_max = lax.optimization_barrier(jnp.max(scores, axis=-1, keepdims=True))
    row_total = lax.optimization_barrier(jnp.sum(jnp.exp(scores - row_max), axis=-1, keepdims=True))
    log_total = row_max + jnp.log(row_total)
    weights = jnp.exp(scores - log_total).astype(jnp.bfloat16)
    mixture = jnp.einsum('hqk,khd->qhd', weights.astype(jnp.float32), value_rows.astype(jnp.float32))
    return (mixture.astype(jnp.bfloat16), log_total)

def attend_back(queries, key_rows, value_rows, mixture, log_total, grad_mixture, in_band):
    factor = 1.0 / math.sqrt(queries.shape[-1])
    scores = masked_scores(queries, key_rows, in_band)
    probability = jnp.exp(scores - log_total)
    prob_low = probability.astype(jnp.bfloat16).astype(jnp.float32)
    grad_in = grad_mixture.astype(jnp.float32)
    grad_values = jnp.einsum('hqk,qhd->khd', prob_low, grad_in)
    grad_probs = jnp.einsum('qhd,khd->hqk', grad_in, value_rows.astype(jnp.float32))
    delta_sum = jnp.transpose(lax.optimization_barrier(jnp.sum(grad_in * mixture.astype(jnp.float32), axis=-1)))[:, :, None]
    grad_scores = (probability * (grad_probs - delta_sum) * factor).astype(jnp.bfloat16).astype(jnp.float32)
    grad_queries = jnp.einsum('hqk,khd->qhd', grad_scores, key_rows.astype(jnp.float32))
    grad_keys = jnp.einsum('hqk,qhd->khd', grad_scores, queries.astype(jnp.float32))
    return (grad_queries, grad_keys, grad_values)

def reference(block_input, attn_gain, qkv_weight, attn_weight, mlp_gain, inner_weight, outer_weight, output_grad):
    cosine_table, sine_table = rope_tables(LEN, HD)
    position = jnp.arange(LEN, dtype=jnp.int32)
    in_band = jnp.abs(position[:, None] - position[None, :]) <= WINDOW // 2

    def one_sequence(running, item_pair):
        source, upstream = item_pair
        values = source.astype(jnp.float32)
        normed_attn, rescale_attn = norm_stats(values)
        low_attn = (normed_attn * attn_gain).astype(jnp.bfloat16)
        qkv_rows = jnp.dot(low_attn, qkv_weight, preferred_element_type=jnp.float32).astype(jnp.bfloat16)
        qkv_rows = qkv_rows.reshape(LEN, 3, HEADS, HD)
        queries = rotate(qkv_rows[:, 0].astype(jnp.float32), cosine_table, sine_table).astype(jnp.bfloat16)
        key_rows = rotate(qkv_rows[:, 1].astype(jnp.float32), cosine_table, sine_table).astype(jnp.bfloat16)
        value_rows = qkv_rows[:, 2]
        mixture, log_total = attend(queries, key_rows, value_rows, in_band)
        mixture_flat = mixture.reshape(LEN, D)
        residual = values + jnp.dot(mixture_flat, attn_weight, preferred_element_type=jnp.float32)
        normed_mlp, rescale_mlp = norm_stats(residual)
        low_mlp = (normed_mlp * mlp_gain).astype(jnp.bfloat16)
        gate_up = jnp.dot(low_mlp, inner_weight, preferred_element_type=jnp.float32)
        gate_part = gate_up[:, :FF]
        up_part = gate_up[:, FF:]
        activated, derivative = gelu_parts(gate_part)
        hidden = (activated * up_part).astype(jnp.bfloat16)
        result = residual + jnp.dot(hidden, outer_weight, preferred_element_type=jnp.float32)
        grad_hidden = jnp.dot(upstream, outer_weight.T, preferred_element_type=jnp.float32)
        outer_term = jnp.dot(hidden.T, upstream, preferred_element_type=jnp.float32)
        grad_gate_up = jnp.concatenate([grad_hidden * up_part * derivative, grad_hidden * activated], axis=1).astype(jnp.bfloat16)
        grad_low_mlp = jnp.dot(grad_gate_up, inner_weight.T, preferred_element_type=jnp.float32)
        inner_term = jnp.dot(low_mlp.T, grad_gate_up, preferred_element_type=jnp.float32)
        mlp_gain_term = lax.optimization_barrier(jnp.sum(grad_low_mlp * normed_mlp, axis=0))
        grad_residual = upstream.astype(jnp.float32) + norm_back(grad_low_mlp, normed_mlp, rescale_mlp, mlp_gain)
        grad_branch = grad_residual.astype(jnp.bfloat16)
        grad_mixture = jnp.dot(grad_branch, attn_weight.T, preferred_element_type=jnp.float32).astype(jnp.bfloat16)
        attn_term = jnp.dot(mixture_flat.T, grad_branch, preferred_element_type=jnp.float32)
        grad_queries, grad_keys, grad_values = attend_back(queries, key_rows, value_rows, mixture, log_total, grad_mixture.reshape(LEN, HEADS, HD), in_band)
        grad_queries = rotate_back(grad_queries, cosine_table, sine_table).astype(jnp.bfloat16)
        grad_keys = rotate_back(grad_keys, cosine_table, sine_table).astype(jnp.bfloat16)
        grad_values = grad_values.astype(jnp.bfloat16)
        grad_qkv = jnp.stack([grad_queries, grad_keys, grad_values], axis=1).reshape(LEN, 3 * D)
        grad_low_attn = jnp.dot(grad_qkv, qkv_weight.T, preferred_element_type=jnp.float32)
        qkv_term = jnp.dot(low_attn.T, grad_qkv, preferred_element_type=jnp.float32)
        attn_gain_term = lax.optimization_barrier(jnp.sum(grad_low_attn * normed_attn, axis=0))
        grad_input = grad_residual + norm_back(grad_low_attn, normed_attn, rescale_attn, attn_gain)
        updated = (running[0] + attn_gain_term, running[1] + qkv_term, running[2] + attn_term, running[3] + mlp_gain_term, running[4] + inner_term, running[5] + outer_term)
        return (updated, (result, grad_input))
    start = (jnp.zeros((D,), jnp.float32), jnp.zeros((D, 3 * D), jnp.float32), jnp.zeros((D, D), jnp.float32), jnp.zeros((D,), jnp.float32), jnp.zeros((D, 2 * FF), jnp.float32), jnp.zeros((FF, D), jnp.float32))
    sources = jnp.transpose(block_input, (1, 0, 2))
    upstreams = jnp.transpose(output_grad, (1, 0, 2))
    totals, outputs = lax.scan(one_sequence, start, (sources, upstreams))
    block_output = jnp.transpose(outputs[0], (1, 0, 2))
    input_grad = jnp.transpose(outputs[1], (1, 0, 2))
    return (block_output, input_grad, totals[0], totals[1], totals[2], totals[3], totals[4], totals[5])
```

```python
import math

import jax
import jax.numpy as jnp
from jax import lax
from jax.experimental import pallas as pl
from jax.experimental.pallas import tpu as pltpu
from jax.sharding import PartitionSpec as P

HD = 64
WINDOW = 128


epsilon = 1e-05
rope_base = 10000.0


def rope_tables(length, size):
    half_size = size // 2
    frequency = rope_base ** (-(2.0 * jnp.arange(half_size, dtype=jnp.float32)) / size)
    angles = jnp.arange(length, dtype=jnp.float32)[:, None] * frequency[None, :]
    cosine_table = jnp.concatenate([jnp.cos(angles), jnp.cos(angles)], axis=1)
    sine_table = jnp.concatenate([jnp.sin(angles), jnp.sin(angles)], axis=1)
    return (cosine_table[:, None, :], sine_table[:, None, :])


def rotate(values, cosine_table, sine_table):
    half_size = values.shape[-1] // 2
    turned = jnp.concatenate([-values[..., half_size:], values[..., :half_size]], axis=-1)
    return values * cosine_table + turned * sine_table


def rotate_back(grads, cosine_table, sine_table):
    half_size = grads.shape[-1] // 2
    scaled = grads * sine_table
    turned = jnp.concatenate([scaled[..., half_size:], -scaled[..., :half_size]], axis=-1)
    return grads * cosine_table + turned


def gelu_parts(gate_part):
    cumulative = 0.5 * (1.0 + lax.erf(gate_part * 0.7071067811865476))
    density = jnp.exp(-0.5 * gate_part * gate_part) * 0.3989422804014327
    return (gate_part * cumulative, cumulative + gate_part * density)


def norm_forward(values, gain):
    width = values.shape[1] * lax.axis_size("gy")
    totals, squares = lax.psum((jnp.sum(values, axis=1), jnp.sum(values * values, axis=1)), "gy")
    center = (totals / width)[:, None]
    spread = (squares / width)[:, None] - center * center
    rescale = lax.rsqrt(spread + epsilon)
    normed = (values - center) * rescale
    return (normed, rescale, (normed * gain).astype(jnp.bfloat16))


def norm_backward(grads, normed, rescale, gain):
    width = grads.shape[1] * lax.axis_size("gy")
    scaled = grads * gain
    first_sum, second = lax.psum((jnp.sum(scaled, axis=1), jnp.sum(scaled * normed, axis=1)), "gy")
    return rescale * (scaled - first_sum[:, None] / width - normed * (second[:, None] / width))


def project(inputs, weight, groups):
    partial_value = jnp.dot(inputs, weight, preferred_element_type=jnp.float32)
    grouped = partial_value.reshape(
        partial_value.shape[0], groups, partial_value.shape[1] // groups
    )
    return lax.psum_scatter(grouped, "gy", scatter_dimension=2, tiled=True)


def widen(grads):
    whole_grad = lax.all_gather(grads, "gy", axis=2, tiled=True)
    return whole_grad.reshape(whole_grad.shape[0], whole_grad.shape[1] * whole_grad.shape[2])


def back_product(full_grad, weight):
    return lax.dot_general(
        full_grad, weight, (((1,), (1,)), ((), ())), preferred_element_type=jnp.float32
    )


def weight_term(inputs, full_grad):
    return lax.dot_general(
        inputs, full_grad, (((0,), (0,)), ((), ())), preferred_element_type=jnp.float32
    )


def to_sequences(blocks):
    return lax.all_to_all(blocks, "gx", split_axis=1, concat_axis=0, tiled=True)


def to_tokens(blocks):
    return lax.all_to_all(blocks, "gx", split_axis=0, concat_axis=1, tiled=True)


def masked_scores(queries, key_rows, in_band):
    factor = 1.0 / math.sqrt(queries.shape[-1])
    scores = (
        jnp.einsum("qhd,khd->hqk", queries, key_rows, preferred_element_type=jnp.float32) * factor
    )
    return jnp.where(in_band[None], scores, -jnp.inf)


def attend_forward(packed, head_count, cosine_table, sine_table, in_band):
    length = packed.shape[0]
    pieces = packed.reshape(length, 3, head_count, HD)
    queries = rotate(pieces[:, 0].astype(jnp.float32), cosine_table, sine_table).astype(
        jnp.bfloat16
    )
    key_rows = rotate(pieces[:, 1].astype(jnp.float32), cosine_table, sine_table).astype(
        jnp.bfloat16
    )
    value_rows = pieces[:, 2]
    scores = masked_scores(queries, key_rows, in_band)
    row_max = jnp.max(scores, axis=-1, keepdims=True)
    row_total = jnp.sum(jnp.exp(scores - row_max), axis=-1, keepdims=True)
    log_total = row_max + jnp.log(row_total)
    weights = jnp.exp(scores - log_total).astype(jnp.bfloat16)
    mixture = jnp.einsum(
        "hqk,khd->qhd", weights, value_rows, preferred_element_type=jnp.float32
    ).astype(jnp.bfloat16)
    return (mixture.reshape(length, head_count * HD), log_total, queries, key_rows)


def attend_backward(item_list, head_count, cosine_table, sine_table, in_band):
    packed, mixture, log_total, queries, key_rows, grad_mixture = item_list
    length = packed.shape[0]
    factor = 1.0 / math.sqrt(HD)
    value_rows = packed.reshape(length, 3, head_count, HD)[:, 2]
    mixture = mixture.reshape(length, head_count, HD)
    grad_mixture = grad_mixture.reshape(length, head_count, HD)
    scores = masked_scores(queries, key_rows, in_band)
    probability = jnp.exp(scores - log_total)
    prob_low = probability.astype(jnp.bfloat16)
    grad_values = jnp.einsum(
        "hqk,qhd->khd", prob_low, grad_mixture, preferred_element_type=jnp.float32
    )
    grad_probs = jnp.einsum(
        "qhd,khd->hqk", grad_mixture, value_rows, preferred_element_type=jnp.float32
    )
    delta_sum = jnp.sum(grad_mixture.astype(jnp.float32) * mixture.astype(jnp.float32), axis=-1)
    delta_sum = jnp.transpose(delta_sum)[:, :, None]
    grad_scores = (probability * (grad_probs - delta_sum) * factor).astype(jnp.bfloat16)
    grad_queries = jnp.einsum(
        "hqk,khd->qhd", grad_scores, key_rows, preferred_element_type=jnp.float32
    )
    grad_keys = jnp.einsum("hqk,qhd->khd", grad_scores, queries, preferred_element_type=jnp.float32)
    grad_queries = rotate_back(grad_queries, cosine_table, sine_table).astype(jnp.bfloat16)
    grad_keys = rotate_back(grad_keys, cosine_table, sine_table).astype(jnp.bfloat16)
    stacked = jnp.stack([grad_queries, grad_keys, grad_values.astype(jnp.bfloat16)], axis=1)
    return stacked.reshape(length, 3 * head_count * HD)


def on_device_general(
    block_input,
    attn_gain,
    qkv_weight,
    attn_weight,
    mlp_gain,
    inner_weight,
    outer_weight,
    output_grad,
):
    positions, sequences, quarter = block_input.shape
    row_count = positions * sequences
    head_count = quarter // HD
    length = positions * lax.axis_size("gx")
    cosine_table, sine_table = rope_tables(length, HD)
    position = jnp.arange(length, dtype=jnp.int32)
    in_band = jnp.abs(position[:, None] - position[None, :]) <= WINDOW // 2
    wide_qkv, wide_attn, wide_inner, wide_outer = (
        lax.all_gather(qkv_weight, "gx", axis=1, tiled=True),
        lax.all_gather(attn_weight, "gx", axis=1, tiled=True),
        lax.all_gather(inner_weight, "gx", axis=1, tiled=True),
        lax.all_gather(outer_weight, "gx", axis=1, tiled=True),
    )
    values = block_input.reshape(row_count, quarter).astype(jnp.float32)
    normed_attn, rescale_attn, low_attn = norm_forward(values, attn_gain)
    packed = (
        project(low_attn, wide_qkv, 3)
        .astype(jnp.bfloat16)
        .reshape(positions, sequences, 3 * quarter)
    )
    seq_packed = jnp.moveaxis(to_sequences(packed), 1, 0)

    def forward_single(single_seq):
        return attend_forward(single_seq, head_count, cosine_table, sine_table, in_band)

    mixture, log_total, queries, key_rows = lax.map(forward_single, seq_packed)
    mixture_tok = to_tokens(jnp.moveaxis(mixture, 0, 1)).reshape(row_count, quarter)
    residual = values + project(mixture_tok, wide_attn, 1).reshape(row_count, quarter)
    normed_mlp, rescale_mlp, low_mlp = norm_forward(residual, mlp_gain)
    gate_up = project(low_mlp, wide_inner, 2)
    gate_part = gate_up[:, 0]
    up_part = gate_up[:, 1]
    activated, derivative = gelu_parts(gate_part)
    hidden = (activated * up_part).astype(jnp.bfloat16)
    result = residual + project(hidden, wide_outer, 1).reshape(row_count, quarter)
    back_qkv, back_attn, back_inner, back_outer = (
        lax.all_gather(qkv_weight, "gx", axis=1, tiled=True),
        lax.all_gather(attn_weight, "gx", axis=1, tiled=True),
        lax.all_gather(inner_weight, "gx", axis=1, tiled=True),
        lax.all_gather(outer_weight, "gx", axis=1, tiled=True),
    )
    upstream = output_grad.reshape(row_count, quarter)
    full_upstream = widen(upstream[:, None, :])
    grad_hidden = back_product(full_upstream, back_outer)
    outer_term = weight_term(hidden, full_upstream)
    grad_gate_up = jnp.stack(
        [grad_hidden * up_part * derivative, grad_hidden * activated], axis=1
    ).astype(jnp.bfloat16)
    full_gate_up = widen(grad_gate_up)
    grad_low_mlp = back_product(full_gate_up, back_inner)
    inner_term = weight_term(low_mlp, full_gate_up)
    mlp_gain_term = jnp.sum(grad_low_mlp * normed_mlp, axis=0)
    grad_residual = upstream.astype(jnp.float32) + norm_backward(
        grad_low_mlp, normed_mlp, rescale_mlp, mlp_gain
    )
    grad_branch = grad_residual.astype(jnp.bfloat16)
    full_branch = widen(grad_branch[:, None, :])
    grad_mixture = back_product(full_branch, back_attn).astype(jnp.bfloat16)
    attn_term = weight_term(mixture_tok, full_branch)
    seq_grad = jnp.moveaxis(to_sequences(grad_mixture.reshape(positions, sequences, quarter)), 1, 0)

    def backward_single(item_list):
        return attend_backward(item_list, head_count, cosine_table, sine_table, in_band)

    grad_packed = lax.map(
        backward_single, (seq_packed, mixture, log_total, queries, key_rows, seq_grad)
    )
    grad_tokens = to_tokens(jnp.moveaxis(grad_packed, 0, 1)).reshape(row_count, 3, quarter)
    full_qkv = widen(grad_tokens)
    grad_low_attn = back_product(full_qkv, back_qkv)
    qkv_term = weight_term(low_attn, full_qkv)
    attn_gain_term = jnp.sum(grad_low_attn * normed_attn, axis=0)
    grad_input = grad_residual + norm_backward(grad_low_attn, normed_attn, rescale_attn, attn_gain)
    qkv_part, attn_part, inner_part, outer_part = (
        lax.psum_scatter(qkv_term, "gx", scatter_dimension=1, tiled=True),
        lax.psum_scatter(attn_term, "gx", scatter_dimension=1, tiled=True),
        lax.psum_scatter(inner_term, "gx", scatter_dimension=1, tiled=True),
        lax.psum_scatter(outer_term, "gx", scatter_dimension=1, tiled=True),
    )
    attn_gain_sum, mlp_gain_sum = lax.psum((attn_gain_term, mlp_gain_term), "gx")
    return (
        result.reshape(positions, sequences, quarter),
        grad_input.reshape(positions, sequences, quarter),
        attn_gain_sum,
        qkv_part,
        attn_part,
        mlp_gain_sum,
        inner_part,
        outer_part,
    )


LANES = 128
SUBLANES = 8
NEG = -1e30


def rings_fit(args, gx_size, gy_size):
    block_input, _, qkv_weight, attn_weight, _, inner_weight, outer_weight, _ = args
    positions, sequences, quarter = block_input.shape
    length = positions * gx_size
    pair_chunks = 2 * qkv_weight.shape[1] // HD
    return (
        gx_size == 8
        and gy_size == 4
        and sequences == gx_size
        and length % (gy_size * LANES) == 0
        and length // gy_size >= WINDOW // 2
        and quarter % LANES == 0
        and (2 * qkv_weight.shape[1]) % (gy_size * HD) == 0
        and pair_chunks % gy_size == 0
        and attn_weight.shape[0] % (gy_size * HD) == 0
        and attn_weight.shape[1] % LANES == 0
        and outer_weight.shape[1] % LANES == 0
        and inner_weight.shape[1] == outer_weight.shape[0]
    )


def ring_up(piece):
    size = lax.axis_size("gx")
    return lax.ppermute(piece, "gx", [(i, (i + 2) % size) for i in range(size)])


def ring_down(piece):
    size = lax.axis_size("gx")
    return lax.ppermute(piece, "gx", [((i + 2) % size, i) for i in range(size)])


def swap_y(piece):
    return lax.ppermute(piece, "gx", [(i, i ^ 1) for i in range(lax.axis_size("gx"))])


def swap_core(piece):
    return lax.ppermute(piece, "gy", [(i, i ^ 1) for i in range(lax.axis_size("gy"))])


def swap_x(piece):
    return lax.ppermute(piece, "gy", [(i, i ^ 2) for i in range(lax.axis_size("gy"))])


def gather_ring(piece):
    pieces = [piece]
    for _ in range(lax.axis_size("gx") // 2 - 1):
        pieces.append(ring_up(pieces[-1]))
    return pieces


def gather_grid(piece):
    return [[own, swap_y(own)] for own in gather_ring(piece)]


def scatter_ring(chunks):
    running = chunks[-1]
    for chunk in chunks[-2::-1]:
        running = add_low(ring_down(running), chunk)
    return running


def scatter_grid(near, far):
    arrived = swap_y(jnp.stack(far))
    return scatter_ring([add_low(chunk, arrived[d]) for d, chunk in enumerate(near)])


def add_low(one, other):
    return (one.astype(jnp.float32) + other.astype(jnp.float32)).astype(jnp.bfloat16)


def gather_quarters(piece):
    across = swap_x(piece)
    pair = jnp.stack([piece, across])
    other = swap_core(pair)
    return jnp.stack([pair[0], other[0], pair[1], other[1]])


def scatter_quarters(chunks):
    arrived = swap_core(jnp.stack([chunks[1], chunks[3]]))
    across = swap_x(add_low(chunks[2], arrived[1]))
    return (
        chunks[0].astype(jnp.float32)
        + arrived[0].astype(jnp.float32)
        + across.astype(jnp.float32)
    )


def by_xor(blocks, index):
    first, second = (index % 2) == 1, index >= 2
    low = [jnp.where(first, blocks[k ^ 1], blocks[k]) for k in range(4)]
    return [jnp.where(second, low[k ^ 2], low[k]) for k in range(4)]


def to_absolute(values, z_at, y_at):
    rows = values.shape[0]
    depth = lax.axis_size("gx") // 2
    width = values.shape[1] // (2 * depth)
    blocks = values.reshape(rows, depth, 2, width)
    blocks = [blocks[:, d] for d in range(depth)]
    mirrored = [blocks[(-d) % depth] for d in range(depth)]
    ordered = []
    for at in range(depth):
        chosen = mirrored[at]
        for shift in range(1, depth):
            chosen = jnp.where(z_at == shift, mirrored[(at - shift) % depth], chosen)
        near, far = chosen[:, 0], chosen[:, 1]
        ordered += [jnp.where(y_at == 0, near, far), jnp.where(y_at == 0, far, near)]
    return jnp.concatenate(ordered, axis=1)


def to_relative(values, z_at, y_at):
    depth = lax.axis_size("gx") // 2
    width = values.shape[1] // (2 * depth)
    parts = [values[:, k * width : (k + 1) * width] for k in range(2 * depth)]
    ordered = []
    for d in range(depth):
        pair = []
        for e in range(2):
            chosen = parts[2 * ((-d) % depth) + e]
            for shift in range(1, depth):
                chosen = jnp.where(z_at == shift, parts[2 * ((shift - d) % depth) + e], chosen)
            pair.append(chosen)
        ordered += [jnp.where(y_at == 0, pair[e], pair[1 - e]) for e in range(2)]
    return jnp.concatenate(ordered, axis=1)


def spread_gy(blocks):
    return lax.all_to_all(blocks, "gy", split_axis=0, concat_axis=0, tiled=True)


def turn(upper, lower, cosine, sine):
    return upper * cosine - lower * sine, lower * cosine + upper * sine


def turn_back(upper, lower, cosine, sine):
    return upper * cosine + lower * sine, lower * cosine - upper * sine


def key_span(at, blocks, width):
    reach = -(-(WINDOW // 2) // width)
    return max(at - reach, 0), min(at + reach + 1, blocks)


def dot_terms(left, right, left_dim, right_dim):
    return lax.dot_general(
        left, right, (((left_dim,), (right_dim,)), ((), ())), preferred_element_type=jnp.float32
    )


def load_heads(where_ref, packed_ref, cosine_ref, sine_ref, head_count, blocks, width):
    head = pl.program_id(0)
    half = HD // 2
    own = where_ref[3 * head_count]

    def rows_of(kind):
        start = pl.multiple_of(where_ref[kind * head_count + head] * HD, HD)
        pieces = []
        for block in range(blocks):
            at = pl.multiple_of(jnp.bitwise_xor(own, block) * width, width)
            pieces.append(packed_ref[pl.ds(start, HD), pl.ds(at, width)])
        return jnp.concatenate(pieces, axis=1)

    def turned(values):
        values = values.astype(jnp.float32)
        upper, lower = turn(values[:half], values[half:], cosine_ref[...], sine_ref[...])
        return jnp.concatenate([upper, lower], axis=0).astype(jnp.bfloat16)

    return turned(rows_of(0)), turned(rows_of(1)), rows_of(2)


def band_scores(queries, key_rows, at, first, last, width):
    factor = 1.0 / math.sqrt(HD)
    scores = factor * dot_terms(
        key_rows[:, first * width : last * width], queries[:, at * width : (at + 1) * width], 0, 0
    )
    key_at = first * width + lax.broadcasted_iota(jnp.int32, scores.shape, 0)
    query_at = at * width + lax.broadcasted_iota(jnp.int32, scores.shape, 1)
    in_band = jnp.abs(key_at - query_at) <= WINDOW // 2
    return jnp.where(in_band, scores, NEG)


def attend_kernel(
    head_count, blocks, where_ref, packed_ref, cosine_ref, sine_ref, mixture_ref, log_ref
):
    width = packed_ref.shape[1] // blocks
    head = pl.program_id(0)
    own = where_ref[3 * head_count]
    queries, key_rows, value_rows = load_heads(
        where_ref, packed_ref, cosine_ref, sine_ref, head_count, blocks, width
    )
    for at in range(blocks):
        first, last = key_span(at, blocks, width)
        scores = band_scores(queries, key_rows, at, first, last, width)
        row_max = jnp.max(scores, axis=0, keepdims=True)
        row_total = jnp.sum(jnp.exp(scores - row_max), axis=0, keepdims=True)
        log_total = row_max + jnp.log(row_total)
        weights = jnp.exp(scores - log_total).astype(jnp.bfloat16)
        mixture = dot_terms(value_rows[:, first * width : last * width], weights, 1, 0)
        to = pl.multiple_of(jnp.bitwise_xor(own, at) * width, width)
        mixture_ref[:, pl.ds(to, width)] = mixture.astype(jnp.bfloat16)
        log_ref[0, :, at * width : (at + 1) * width] = log_total


def attend_back_kernel(
    head_count,
    blocks,
    where_ref,
    packed_ref,
    cosine_ref,
    sine_ref,
    mixture_ref,
    log_ref,
    grad_ref,
    out_ref,
    query_sum,
    key_sum,
    value_sum,
):
    width = packed_ref.shape[1] // blocks
    half = HD // 2
    factor = 1.0 / math.sqrt(HD)
    head = pl.program_id(0)
    own = where_ref[3 * head_count]
    queries, key_rows, value_rows = load_heads(
        where_ref, packed_ref, cosine_ref, sine_ref, head_count, blocks, width
    )
    key_sum[...] = jnp.zeros_like(key_sum)
    value_sum[...] = jnp.zeros_like(value_sum)
    for at in range(blocks):
        first, last = key_span(at, blocks, width)
        low, high = first * width, last * width
        here = slice(at * width, (at + 1) * width)
        source = pl.multiple_of(jnp.bitwise_xor(own, at) * width, width)
        grad_mixture = grad_ref[:, pl.ds(source, width)]
        mixture = mixture_ref[:, pl.ds(source, width)]
        scores = band_scores(queries, key_rows, at, first, last, width)
        probability = jnp.exp(scores - log_ref[0, :, here])
        prob_low = probability.astype(jnp.bfloat16)
        value_sum[:, low:high] += dot_terms(grad_mixture, prob_low, 1, 1)
        grad_probs = dot_terms(value_rows[:, low:high], grad_mixture, 0, 0)
        delta_sum = jnp.sum(
            grad_mixture.astype(jnp.float32) * mixture.astype(jnp.float32), axis=0, keepdims=True
        )
        grad_scores = (probability * (grad_probs - delta_sum) * factor).astype(jnp.bfloat16)
        query_sum[:, here] = dot_terms(key_rows[:, low:high], grad_scores, 1, 0)
        key_sum[:, low:high] += dot_terms(queries[:, here], grad_scores, 1, 1)

    def put(kind, values):
        start = pl.multiple_of(where_ref[kind * head_count + head] * HD, HD)
        for block in range(blocks):
            to = pl.multiple_of(jnp.bitwise_xor(own, block) * width, width)
            out_ref[pl.ds(start, HD), pl.ds(to, width)] = values[
                :, block * width : (block + 1) * width
            ].astype(jnp.bfloat16)

    for kind, total in ((0, query_sum), (1, key_sum)):
        upper, lower = turn_back(total[:half], total[half:], cosine_ref[...], sine_ref[...])
        put(kind, jnp.concatenate([upper, lower], axis=0))
    put(2, value_sum[...])


def attention_specs(head_count, rows, length):
    whole = pl.BlockSpec((rows, length), lambda h, w: (0, 0))
    table = pl.BlockSpec((HD // 2, length), lambda h, w: (0, 0))
    head = pl.BlockSpec((HD, length), lambda h, w: (h, 0))
    logs = pl.BlockSpec((1, 1, length), lambda h, w: (h, 0, 0))
    return whole, table, head, logs


def attend_cost(head_count, length, products):
    return pl.CostEstimate(
        flops=2 * products * head_count * length * 3 * LANES * HD,
        bytes_accessed=8 * head_count * HD * length,
        transcendentals=2 * head_count * length * 3 * LANES,
    )


def attend(where, packed, cosine, sine, head_count, blocks):
    rows, length = packed.shape
    whole, table, head, logs = attention_specs(head_count, rows, length)

    def kernel(*refs):
        attend_kernel(head_count, blocks, *refs)

    return pl.pallas_call(
        kernel,
        out_shape=(
            jax.ShapeDtypeStruct((head_count * HD, length), jnp.bfloat16),
            jax.ShapeDtypeStruct((head_count, 1, length), jnp.float32),
        ),
        grid_spec=pltpu.PrefetchScalarGridSpec(
            num_scalar_prefetch=1,
            grid=(head_count,),
            in_specs=[whole, table, table],
            out_specs=[head, logs],
        ),
        cost_estimate=attend_cost(head_count, length, 2),
        name="attend",
    )(where, packed, cosine, sine)


def attend_back(where, packed, cosine, sine, mixture, logs_in, grad, head_count, blocks):
    rows, length = packed.shape
    whole, table, head, logs = attention_specs(head_count, rows, length)

    def kernel(*refs):
        attend_back_kernel(head_count, blocks, *refs)

    return pl.pallas_call(
        kernel,
        out_shape=jax.ShapeDtypeStruct((rows, length), jnp.bfloat16),
        grid_spec=pltpu.PrefetchScalarGridSpec(
            num_scalar_prefetch=1,
            grid=(head_count,),
            in_specs=[whole, table, table, head, logs, head],
            out_specs=whole,
            scratch_shapes=[pltpu.VMEM((HD, length), jnp.float32)] * 3,
        ),
        cost_estimate=attend_cost(head_count, length, 5),
        name="attend_back",
    )(where, packed, cosine, sine, mixture, logs_in, grad)


def row_norm(values):
    center = jnp.mean(values, axis=1, keepdims=True)
    spread = jnp.mean((values - center) ** 2, axis=1, keepdims=True)
    rescale = lax.rsqrt(spread + epsilon)
    return (values - center) * rescale, rescale


def row_norm_back(grads, normed, rescale, gain):
    scaled = grads * gain
    first_mean = jnp.mean(scaled, axis=1, keepdims=True)
    second_mean = jnp.mean(scaled * normed, axis=1, keepdims=True)
    return rescale * (scaled - first_mean - normed * second_mean)


def whole_gain(gain, gy_at):
    return jnp.concatenate(by_xor(gather_quarters(gain[None, :]), gy_at), axis=1)


def sum_gain(term, gy_at):
    size = lax.axis_size("gx")
    term = term + swap_core(term)
    term = term + swap_x(term)
    width = term.shape[1] // lax.axis_size("gy")
    term = lax.dynamic_slice_in_dim(term, gy_at * width, width, axis=1)
    term = term + swap_y(term)
    term = term + lax.ppermute(term, "gx", [(i, i ^ 2) for i in range(size)])
    term = term + lax.ppermute(term, "gx", [(i, i ^ 4) for i in range(size)])
    return term[0]


def on_device_rings(
    block_input,
    attn_gain,
    qkv_weight,
    attn_weight,
    mlp_gain,
    inner_weight,
    outer_weight,
    output_grad,
):
    positions, sequences, quarter = block_input.shape
    gx_size, gy_size = lax.axis_size("gx"), lax.axis_size("gy")
    gx_at, gy_at = lax.axis_index("gx"), lax.axis_index("gy")
    z_at, y_at = gx_at // 2, gx_at % 2
    depth = gx_size // 2
    length = positions * gx_size
    rows = length // gy_size
    width = quarter * gy_size
    head_count = quarter // HD
    unit_count = outer_weight.shape[0]
    units = -(-unit_count // (gy_size * SUBLANES)) * SUBLANES
    padding = gy_size * units - unit_count
    far_y = y_at == 1
    odd_z = (z_at % 2) == 1

    def whole_sequence(blocks):
        tokens = lax.all_to_all(blocks, "gx", split_axis=1, concat_axis=0, tiled=True)
        tokens = tokens.reshape(gy_size, rows, quarter)
        tokens = jnp.stack(by_xor(tokens, gy_at))
        parts = gather_quarters(tokens)
        parts = [jnp.concatenate([parts[j, f ^ j] for f in range(4)], axis=0) for j in range(4)]
        return jnp.concatenate(by_xor(parts, gy_at), axis=1)

    source = whole_sequence(block_input)

    turned = qkv_weight.T
    other = swap_y(turned)
    pair = jnp.concatenate(
        [jnp.where(far_y, other, turned), jnp.where(far_y, turned, other)], axis=0
    )
    per_device = pair.shape[0] // (gy_size * HD)
    pair = pair.reshape(per_device, gy_size, HD, quarter)
    pair = spread_gy(jnp.moveaxis(pair, 1, 0))
    chunk_rows = per_device * HD
    pair = jnp.concatenate([pair[k].reshape(chunk_rows, quarter) for k in range(4)], axis=1)
    qkv_whole = jnp.concatenate(gather_ring(pair), axis=0)

    attn_blocks = attn_weight.reshape(head_count, HD, attn_weight.shape[1])
    outer_blocks = jnp.pad(outer_weight, ((0, padding), (0, 0)))
    outer_blocks = outer_blocks.reshape(gy_size, units, outer_weight.shape[1])
    both = spread_gy(jnp.concatenate([attn_blocks, outer_blocks], axis=1))
    attn_part = both[:, :HD].reshape(head_count * HD, attn_weight.shape[1])
    outer_part = both[:, HD:].reshape(2, 2, units, outer_weight.shape[1])

    def relate(blocks):
        blocks = [[blocks[p, e] for e in range(2)] for p in range(2)]
        blocks = [[jnp.where(far_y, b[1 - e], b[e]) for e in range(2)] for b in blocks]
        return [[jnp.where(odd_z, blocks[1 - p][e], blocks[p][e]) for e in range(2)] for p in range(2)]

    outer_part = relate(outer_part)
    inner_blocks = jnp.pad(inner_weight.T, ((0, padding), (0, 0)))
    inner_blocks = spread_gy(inner_blocks.reshape(gy_size, units, quarter))
    inner_part = jnp.concatenate([inner_blocks[k] for k in range(4)], axis=1)

    attn_grid = gather_grid(attn_part)
    attn_whole = jnp.concatenate([piece for pieces in attn_grid for piece in pieces], axis=1)
    inner_grid = gather_grid(inner_part)
    inner_whole = jnp.concatenate([piece for pieces in inner_grid for piece in pieces], axis=0)
    outer_grid = gather_grid(jnp.stack([outer_part[p][e] for p in range(2) for e in range(2)]))
    outer_whole = jnp.concatenate(
        [
            jnp.concatenate(
                [
                    outer_grid[d][far][2 * ((p + d) % 2) + (e ^ far)]
                    for d in range(depth)
                    for far in range(2)
                ],
                axis=1,
            )
            for p in range(2)
            for e in range(2)
        ],
        axis=0,
    )
    first_gain, second_gain = whole_gain(attn_gain, gy_at), whole_gain(mlp_gain, gy_at)

    normed_attn, rescale_attn = row_norm(source.astype(jnp.float32))
    low_attn = (normed_attn * first_gain).astype(jnp.bfloat16)
    packed = dot_terms(qkv_whole, low_attn, 1, 1).astype(jnp.bfloat16)
    half = HD // 2
    frequency = rope_base ** (-(2.0 * jnp.arange(half, dtype=jnp.float32)) / HD)
    angles = frequency[:, None] * jnp.arange(length, dtype=jnp.float32)[None, :]
    cosine, sine = jnp.cos(angles), jnp.sin(angles)
    order = jnp.arange(3 * head_count, dtype=jnp.int32)
    place = lax.rem(z_at - order // per_device + depth, depth) * per_device + order % per_device
    where = jnp.concatenate([place, gy_at[None]]).astype(jnp.int32)
    mixture, log_total = attend(where, packed, cosine, sine, head_count, gy_size)

    def reduce_rows(partial_sum):
        chunks = partial_sum.astype(jnp.bfloat16).reshape(gy_size, rows, width)
        return scatter_quarters(chunks)

    def gather_rows(piece):
        return gather_quarters(piece).reshape(length, width)

    attended = reduce_rows(dot_terms(mixture, attn_whole, 0, 0))
    residual = source[:rows].astype(jnp.float32) + to_absolute(attended, z_at, y_at)

    normed_mlp, rescale_mlp = row_norm(residual)
    low_mlp = gather_rows((normed_mlp * second_gain).astype(jnp.bfloat16))
    gate_up = dot_terms(inner_whole, low_mlp, 1, 1).reshape(depth, 2 * units, length)
    first_is_gate = z_at < depth // 2
    second_is_gate = lax.rem(z_at + depth - 1, depth) < depth // 2
    is_gate = jnp.stack([first_is_gate, second_is_gate])[:, None, None]
    gate_part = jnp.where(is_gate, gate_up[:2], gate_up[2:])
    up_part = jnp.where(is_gate, gate_up[2:], gate_up[:2])
    activated, derivative = gelu_parts(gate_part)
    hidden = (activated * up_part).astype(jnp.bfloat16).reshape(4 * units, length)
    projected = reduce_rows(dot_terms(hidden, outer_whole, 0, 0))
    result = residual + to_absolute(projected, z_at, y_at)

    upstream = whole_sequence(output_grad)
    upstream_turned = to_relative(upstream, z_at, y_at)
    grad_hidden = dot_terms(outer_whole, upstream_turned, 1, 1).reshape(2, 2 * units, length)
    grad_gate = (grad_hidden * up_part * derivative).astype(jnp.bfloat16)
    grad_up = (grad_hidden * activated).astype(jnp.bfloat16)
    grad_gate_up = jnp.concatenate(
        [jnp.where(is_gate, grad_gate, grad_up), jnp.where(is_gate, grad_up, grad_gate)], axis=0
    ).reshape(2 * depth * units, length)

    grad_low_mlp = reduce_rows(dot_terms(grad_gate_up, inner_whole, 0, 0))
    grad_residual = upstream[:rows].astype(jnp.float32) + row_norm_back(
        grad_low_mlp, normed_mlp, rescale_mlp, second_gain
    )
    mlp_gain_term = jnp.sum(grad_low_mlp * normed_mlp, axis=0, keepdims=True)

    outer_term = dot_terms(hidden, upstream_turned, 1, 0).astype(jnp.bfloat16)
    outer_term = outer_term.reshape(2, 2, units, depth, 2, outer_weight.shape[1])

    def outer_chunk(d, far):
        return jnp.concatenate(
            [outer_term[(p + d) % 2, e ^ far, :, d, far] for p in range(2) for e in range(2)],
            axis=0,
        )

    outer_sum = scatter_grid(
        [outer_chunk(d, 0) for d in range(depth)], [outer_chunk(d, 1) for d in range(depth)]
    )
    outer_sum = relate(outer_sum.reshape(2, 2, units, outer_weight.shape[1]))
    outer_sum = spread_gy(jnp.stack([outer_sum[p][e] for p in range(2) for e in range(2)]))
    outer_out = outer_sum.reshape(gy_size * units, outer_weight.shape[1])[:unit_count]

    inner_term = dot_terms(grad_gate_up, low_mlp, 1, 0).astype(jnp.bfloat16)
    inner_term = inner_term.reshape(depth, 2, units, width)
    inner_sum = scatter_grid(
        [inner_term[d, 0] for d in range(depth)], [inner_term[d, 1] for d in range(depth)]
    )
    inner_sum = jnp.moveaxis(inner_sum.reshape(units, gy_size, quarter), 1, 0)
    inner_sum = spread_gy(inner_sum).reshape(gy_size * units, quarter)[:unit_count]
    inner_out = inner_sum.T

    branch = to_relative(grad_residual.astype(jnp.bfloat16), z_at, y_at)
    branch = gather_rows(branch)
    grad_mixture = dot_terms(attn_whole, branch, 1, 1).astype(jnp.bfloat16)
    attn_term = dot_terms(mixture, branch, 1, 0).astype(jnp.bfloat16)
    attn_term = attn_term.reshape(head_count * HD, depth, 2, attn_weight.shape[1])
    attn_sum = scatter_grid(
        [attn_term[:, d, 0] for d in range(depth)], [attn_term[:, d, 1] for d in range(depth)]
    )
    attn_out = spread_gy(attn_sum.reshape(head_count, HD, attn_weight.shape[1]))
    attn_out = attn_out.reshape(head_count * HD, attn_weight.shape[1])

    grad_packed = attend_back(
        where, packed, cosine, sine, mixture, log_total, grad_mixture, head_count, gy_size
    )
    grad_low_attn = reduce_rows(dot_terms(grad_packed, qkv_whole, 0, 0))
    qkv_term = dot_terms(grad_packed, low_attn, 1, 0).astype(jnp.bfloat16)
    qkv_term = qkv_term.reshape(depth, chunk_rows, width)
    qkv_sum = scatter_ring([qkv_term[d] for d in range(depth)])
    qkv_sum = jnp.moveaxis(qkv_sum.reshape(chunk_rows, gy_size, quarter), 1, 0)
    qkv_sum = spread_gy(qkv_sum).reshape(gy_size, per_device, HD, quarter)
    qkv_sum = jnp.moveaxis(qkv_sum, 0, 1).reshape(2, qkv_weight.shape[1], quarter)
    kept = jnp.where(far_y, qkv_sum[1], qkv_sum[0])
    sent = swap_y(jnp.where(far_y, qkv_sum[0], qkv_sum[1]))
    qkv_out = (kept.astype(jnp.float32) + sent.astype(jnp.float32)).T

    normed_rows, rescale_rows = normed_attn[:rows], rescale_attn[:rows]
    attn_gain_term = jnp.sum(grad_low_attn * normed_rows, axis=0, keepdims=True)
    grad_input = grad_residual + row_norm_back(grad_low_attn, normed_rows, rescale_rows, first_gain)

    def to_placement(values):
        parts = values.astype(jnp.bfloat16).reshape(rows, gy_size, quarter)
        tokens = spread_gy(jnp.moveaxis(parts, 1, 0)).reshape(length, 1, quarter)
        blocks = lax.all_to_all(tokens, "gx", split_axis=0, concat_axis=1, tiled=True)
        return blocks.astype(jnp.float32)

    return (
        to_placement(result),
        to_placement(grad_input),
        sum_gain(attn_gain_term, gy_at),
        qkv_out,
        attn_out.astype(jnp.float32),
        sum_gain(mlp_gain_term, gy_at),
        inner_out.astype(jnp.float32),
        outer_out.astype(jnp.float32),
    )


def solution(mesh):
    def on_device(*args):
        if rings_fit(args, mesh.shape["gx"], mesh.shape["gy"]):
            return on_device_rings(*args)
        return on_device_general(*args)

    return jax.shard_map(
        on_device,
        mesh=mesh,
        in_specs=(
            P("gx", None, "gy"),
            P("gy"),
            P("gy", "gx"),
            P("gy", "gx"),
            P("gy"),
            P("gy", "gx"),
            P("gy", "gx"),
            P("gx", None, "gy"),
        ),
        out_specs=(
            P("gx", None, "gy"),
            P("gx", None, "gy"),
            P("gy"),
            P("gy", "gx"),
            P("gy", "gx"),
            P("gy"),
            P("gy", "gx"),
            P("gy", "gx"),
        ),
        check_vma=False,
    )
```

```python
import math

import jax
import jax.numpy as jnp
from jax import lax
from jax.experimental import pallas as pl
from jax.experimental.pallas import tpu as pltpu
from jax.sharding import PartitionSpec as P

HD = 64
WINDOW = 128


epsilon = 1e-05
rope_base = 10000.0


def rope_tables(length, size):
    half_size = size // 2
    frequency = rope_base ** (-(2.0 * jnp.arange(half_size, dtype=jnp.float32)) / size)
    angles = jnp.arange(length, dtype=jnp.float32)[:, None] * frequency[None, :]
    cosine_table = jnp.concatenate([jnp.cos(angles), jnp.cos(angles)], axis=1)
    sine_table = jnp.concatenate([jnp.sin(angles), jnp.sin(angles)], axis=1)
    return (cosine_table[:, None, :], sine_table[:, None, :])


def rotate(values, cosine_table, sine_table):
    half_size = values.shape[-1] // 2
    turned = jnp.concatenate([-values[..., half_size:], values[..., :half_size]], axis=-1)
    return values * cosine_table + turned * sine_table


def rotate_back(grads, cosine_table, sine_table):
    half_size = grads.shape[-1] // 2
    scaled = grads * sine_table
    turned = jnp.concatenate([scaled[..., half_size:], -scaled[..., :half_size]], axis=-1)
    return grads * cosine_table + turned


def gelu_parts(gate_part):
    cumulative = 0.5 * (1.0 + lax.erf(gate_part * 0.7071067811865476))
    density = jnp.exp(-0.5 * gate_part * gate_part) * 0.3989422804014327
    return (gate_part * cumulative, cumulative + gate_part * density)


def norm_forward(values, gain):
    width = values.shape[1] * lax.axis_size("gy")
    totals, squares = lax.psum((jnp.sum(values, axis=1), jnp.sum(values * values, axis=1)), "gy")
    center = (totals / width)[:, None]
    spread = (squares / width)[:, None] - center * center
    rescale = lax.rsqrt(spread + epsilon)
    normed = (values - center) * rescale
    return (normed, rescale, (normed * gain).astype(jnp.bfloat16))


def norm_backward(grads, normed, rescale, gain):
    width = grads.shape[1] * lax.axis_size("gy")
    scaled = grads * gain
    first_sum, second = lax.psum((jnp.sum(scaled, axis=1), jnp.sum(scaled * normed, axis=1)), "gy")
    return rescale * (scaled - first_sum[:, None] / width - normed * (second[:, None] / width))


def project(inputs, weight, groups):
    partial_value = jnp.dot(inputs, weight, preferred_element_type=jnp.float32)
    grouped = partial_value.reshape(
        partial_value.shape[0], groups, partial_value.shape[1] // groups
    )
    return lax.psum_scatter(grouped, "gy", scatter_dimension=2, tiled=True)


def widen(grads):
    whole_grad = lax.all_gather(grads, "gy", axis=2, tiled=True)
    return whole_grad.reshape(whole_grad.shape[0], whole_grad.shape[1] * whole_grad.shape[2])


def back_product(full_grad, weight):
    return lax.dot_general(
        full_grad, weight, (((1,), (1,)), ((), ())), preferred_element_type=jnp.float32
    )


def weight_term(inputs, full_grad):
    return lax.dot_general(
        inputs, full_grad, (((0,), (0,)), ((), ())), preferred_element_type=jnp.float32
    )


def to_sequences(blocks):
    return lax.all_to_all(blocks, "gx", split_axis=1, concat_axis=0, tiled=True)


def to_tokens(blocks):
    return lax.all_to_all(blocks, "gx", split_axis=0, concat_axis=1, tiled=True)


def masked_scores(queries, key_rows, in_band):
    factor = 1.0 / math.sqrt(queries.shape[-1])
    scores = (
        jnp.einsum("qhd,khd->hqk", queries, key_rows, preferred_element_type=jnp.float32) * factor
    )
    return jnp.where(in_band[None], scores, -jnp.inf)


def attend_forward(packed, head_count, cosine_table, sine_table, in_band):
    length = packed.shape[0]
    pieces = packed.reshape(length, 3, head_count, HD)
    queries = rotate(pieces[:, 0].astype(jnp.float32), cosine_table, sine_table).astype(
        jnp.bfloat16
    )
    key_rows = rotate(pieces[:, 1].astype(jnp.float32), cosine_table, sine_table).astype(
        jnp.bfloat16
    )
    value_rows = pieces[:, 2]
    scores = masked_scores(queries, key_rows, in_band)
    row_max = jnp.max(scores, axis=-1, keepdims=True)
    row_total = jnp.sum(jnp.exp(scores - row_max), axis=-1, keepdims=True)
    log_total = row_max + jnp.log(row_total)
    weights = jnp.exp(scores - log_total).astype(jnp.bfloat16)
    mixture = jnp.einsum(
        "hqk,khd->qhd", weights, value_rows, preferred_element_type=jnp.float32
    ).astype(jnp.bfloat16)
    return (mixture.reshape(length, head_count * HD), log_total, queries, key_rows)


def attend_backward(item_list, head_count, cosine_table, sine_table, in_band):
    packed, mixture, log_total, queries, key_rows, grad_mixture = item_list
    length = packed.shape[0]
    factor = 1.0 / math.sqrt(HD)
    value_rows = packed.reshape(length, 3, head_count, HD)[:, 2]
    mixture = mixture.reshape(length, head_count, HD)
    grad_mixture = grad_mixture.reshape(length, head_count, HD)
    scores = masked_scores(queries, key_rows, in_band)
    probability = jnp.exp(scores - log_total)
    prob_low = probability.astype(jnp.bfloat16)
    grad_values = jnp.einsum(
        "hqk,qhd->khd", prob_low, grad_mixture, preferred_element_type=jnp.float32
    )
    grad_probs = jnp.einsum(
        "qhd,khd->hqk", grad_mixture, value_rows, preferred_element_type=jnp.float32
    )
    delta_sum = jnp.sum(grad_mixture.astype(jnp.float32) * mixture.astype(jnp.float32), axis=-1)
    delta_sum = jnp.transpose(delta_sum)[:, :, None]
    grad_scores = (probability * (grad_probs - delta_sum) * factor).astype(jnp.bfloat16)
    grad_queries = jnp.einsum(
        "hqk,khd->qhd", grad_scores, key_rows, preferred_element_type=jnp.float32
    )
    grad_keys = jnp.einsum("hqk,qhd->khd", grad_scores, queries, preferred_element_type=jnp.float32)
    grad_queries = rotate_back(grad_queries, cosine_table, sine_table).astype(jnp.bfloat16)
    grad_keys = rotate_back(grad_keys, cosine_table, sine_table).astype(jnp.bfloat16)
    stacked = jnp.stack([grad_queries, grad_keys, grad_values.astype(jnp.bfloat16)], axis=1)
    return stacked.reshape(length, 3 * head_count * HD)


def on_device_general(
    block_input,
    attn_gain,
    qkv_weight,
    attn_weight,
    mlp_gain,
    inner_weight,
    outer_weight,
    output_grad,
):
    positions, sequences, quarter = block_input.shape
    row_count = positions * sequences
    head_count = quarter // HD
    length = positions * lax.axis_size("gx")
    cosine_table, sine_table = rope_tables(length, HD)
    position = jnp.arange(length, dtype=jnp.int32)
    in_band = jnp.abs(position[:, None] - position[None, :]) <= WINDOW // 2
    wide_qkv, wide_attn, wide_inner, wide_outer = (
        lax.all_gather(qkv_weight, "gx", axis=1, tiled=True),
        lax.all_gather(attn_weight, "gx", axis=1, tiled=True),
        lax.all_gather(inner_weight, "gx", axis=1, tiled=True),
        lax.all_gather(outer_weight, "gx", axis=1, tiled=True),
    )
    values = block_input.reshape(row_count, quarter).astype(jnp.float32)
    normed_attn, rescale_attn, low_attn = norm_forward(values, attn_gain)
    packed = (
        project(low_attn, wide_qkv, 3)
        .astype(jnp.bfloat16)
        .reshape(positions, sequences, 3 * quarter)
    )
    seq_packed = jnp.moveaxis(to_sequences(packed), 1, 0)

    def forward_single(single_seq):
        return attend_forward(single_seq, head_count, cosine_table, sine_table, in_band)

    mixture, log_total, queries, key_rows = lax.map(forward_single, seq_packed)
    mixture_tok = to_tokens(jnp.moveaxis(mixture, 0, 1)).reshape(row_count, quarter)
    residual = values + project(mixture_tok, wide_attn, 1).reshape(row_count, quarter)
    normed_mlp, rescale_mlp, low_mlp = norm_forward(residual, mlp_gain)
    gate_up = project(low_mlp, wide_inner, 2)
    gate_part = gate_up[:, 0]
    up_part = gate_up[:, 1]
    activated, derivative = gelu_parts(gate_part)
    hidden = (activated * up_part).astype(jnp.bfloat16)
    result = residual + project(hidden, wide_outer, 1).reshape(row_count, quarter)
    back_qkv, back_attn, back_inner, back_outer = (
        lax.all_gather(qkv_weight, "gx", axis=1, tiled=True),
        lax.all_gather(attn_weight, "gx", axis=1, tiled=True),
        lax.all_gather(inner_weight, "gx", axis=1, tiled=True),
        lax.all_gather(outer_weight, "gx", axis=1, tiled=True),
    )
    upstream = output_grad.reshape(row_count, quarter)
    full_upstream = widen(upstream[:, None, :])
    grad_hidden = back_product(full_upstream, back_outer)
    outer_term = weight_term(hidden, full_upstream)
    grad_gate_up = jnp.stack(
        [grad_hidden * up_part * derivative, grad_hidden * activated], axis=1
    ).astype(jnp.bfloat16)
    full_gate_up = widen(grad_gate_up)
    grad_low_mlp = back_product(full_gate_up, back_inner)
    inner_term = weight_term(low_mlp, full_gate_up)
    mlp_gain_term = jnp.sum(grad_low_mlp * normed_mlp, axis=0)
    grad_residual = upstream.astype(jnp.float32) + norm_backward(
        grad_low_mlp, normed_mlp, rescale_mlp, mlp_gain
    )
    grad_branch = grad_residual.astype(jnp.bfloat16)
    full_branch = widen(grad_branch[:, None, :])
    grad_mixture = back_product(full_branch, back_attn).astype(jnp.bfloat16)
    attn_term = weight_term(mixture_tok, full_branch)
    seq_grad = jnp.moveaxis(to_sequences(grad_mixture.reshape(positions, sequences, quarter)), 1, 0)

    def backward_single(item_list):
        return attend_backward(item_list, head_count, cosine_table, sine_table, in_band)

    grad_packed = lax.map(
        backward_single, (seq_packed, mixture, log_total, queries, key_rows, seq_grad)
    )
    grad_tokens = to_tokens(jnp.moveaxis(grad_packed, 0, 1)).reshape(row_count, 3, quarter)
    full_qkv = widen(grad_tokens)
    grad_low_attn = back_product(full_qkv, back_qkv)
    qkv_term = weight_term(low_attn, full_qkv)
    attn_gain_term = jnp.sum(grad_low_attn * normed_attn, axis=0)
    grad_input = grad_residual + norm_backward(grad_low_attn, normed_attn, rescale_attn, attn_gain)
    qkv_part, attn_part, inner_part, outer_part = (
        lax.psum_scatter(qkv_term, "gx", scatter_dimension=1, tiled=True),
        lax.psum_scatter(attn_term, "gx", scatter_dimension=1, tiled=True),
        lax.psum_scatter(inner_term, "gx", scatter_dimension=1, tiled=True),
        lax.psum_scatter(outer_term, "gx", scatter_dimension=1, tiled=True),
    )
    attn_gain_sum, mlp_gain_sum = lax.psum((attn_gain_term, mlp_gain_term), "gx")
    return (
        result.reshape(positions, sequences, quarter),
        grad_input.reshape(positions, sequences, quarter),
        attn_gain_sum,
        qkv_part,
        attn_part,
        mlp_gain_sum,
        inner_part,
        outer_part,
    )


LANES = 128
SUBLANES = 8
NEG = -1e30


def rings_fit(args, gx_size, gy_size):
    block_input, _, qkv_weight, attn_weight, _, inner_weight, outer_weight, _ = args
    positions, sequences, quarter = block_input.shape
    length = positions * gx_size
    pair_chunks = 2 * qkv_weight.shape[1] // HD
    return (
        gx_size == 8
        and gy_size == 4
        and sequences == gx_size
        and length % (gy_size * LANES) == 0
        and length // gy_size >= WINDOW // 2
        and quarter % LANES == 0
        and (2 * qkv_weight.shape[1]) % (gy_size * HD) == 0
        and pair_chunks % gy_size == 0
        and attn_weight.shape[0] % (gy_size * HD) == 0
        and attn_weight.shape[1] % LANES == 0
        and outer_weight.shape[1] % LANES == 0
        and inner_weight.shape[1] == outer_weight.shape[0]
    )


def ring_up(piece):
    size = lax.axis_size("gx")
    return lax.ppermute(piece, "gx", [(i, (i + 2) % size) for i in range(size)])


def ring_down(piece):
    size = lax.axis_size("gx")
    return lax.ppermute(piece, "gx", [((i + 2) % size, i) for i in range(size)])


def swap_y(piece):
    return lax.ppermute(piece, "gx", [(i, i ^ 1) for i in range(lax.axis_size("gx"))])


def swap_core(piece):
    return lax.ppermute(piece, "gy", [(i, i ^ 1) for i in range(lax.axis_size("gy"))])


def swap_x(piece):
    return lax.ppermute(piece, "gy", [(i, i ^ 2) for i in range(lax.axis_size("gy"))])


def after(value, *milestones):
    return lax.optimization_barrier((value, *milestones))[0]


def gather_ring(piece, milestones=((), (), ())):
    pieces = [piece]
    for step in range(lax.axis_size("gx") // 2 - 1):
        pieces.append(ring_up(after(pieces[-1], *milestones[step])))
    return pieces


def scatter_ring(chunks, milestones=((), (), (), ())):
    running = chunks[-1]
    for step, chunk in enumerate(chunks[-2::-1]):
        running = ring_down(running)
        running = add_low(after(running, *milestones[step]), chunk)
    return running


def add_low(one, other):
    return (one.astype(jnp.float32) + other.astype(jnp.float32)).astype(jnp.bfloat16)


def gather_quarters(piece):
    across = swap_x(piece)
    pair = jnp.stack([piece, across])
    other = swap_core(pair)
    return jnp.stack([pair[0], other[0], pair[1], other[1]])


def scatter_quarters(chunks):
    arrived = swap_core(jnp.stack([chunks[1], chunks[3]]))
    across = swap_x(add_low(chunks[2], arrived[1]))
    return (
        chunks[0].astype(jnp.float32)
        + arrived[0].astype(jnp.float32)
        + across.astype(jnp.float32)
    )


def by_xor(blocks, index):
    first, second = (index % 2) == 1, index >= 2
    low = [jnp.where(first, blocks[k ^ 1], blocks[k]) for k in range(4)]
    return [jnp.where(second, low[k ^ 2], low[k]) for k in range(4)]


def to_absolute(values, z_at, y_at):
    rows = values.shape[0]
    depth = lax.axis_size("gx") // 2
    width = values.shape[1] // (2 * depth)
    blocks = values.reshape(rows, depth, 2, width)
    blocks = [blocks[:, d] for d in range(depth)]
    mirrored = [blocks[(-d) % depth] for d in range(depth)]
    ordered = []
    for at in range(depth):
        chosen = mirrored[at]
        for shift in range(1, depth):
            chosen = jnp.where(z_at == shift, mirrored[(at - shift) % depth], chosen)
        near, far = chosen[:, 0], chosen[:, 1]
        ordered += [jnp.where(y_at == 0, near, far), jnp.where(y_at == 0, far, near)]
    return jnp.concatenate(ordered, axis=1)


def to_relative(values, z_at, y_at):
    depth = lax.axis_size("gx") // 2
    width = values.shape[1] // (2 * depth)
    parts = [values[:, k * width : (k + 1) * width] for k in range(2 * depth)]
    ordered = []
    for d in range(depth):
        pair = []
        for e in range(2):
            chosen = parts[2 * ((-d) % depth) + e]
            for shift in range(1, depth):
                chosen = jnp.where(z_at == shift, parts[2 * ((shift - d) % depth) + e], chosen)
            pair.append(chosen)
        ordered += [jnp.where(y_at == 0, pair[e], pair[1 - e]) for e in range(2)]
    return jnp.concatenate(ordered, axis=1)


def spread_gy(blocks):
    return lax.all_to_all(blocks, "gy", split_axis=0, concat_axis=0, tiled=True)


def turn(upper, lower, cosine, sine):
    return upper * cosine - lower * sine, lower * cosine + upper * sine


def turn_back(upper, lower, cosine, sine):
    return upper * cosine + lower * sine, lower * cosine - upper * sine


def key_span(at, blocks, width):
    reach = -(-(WINDOW // 2) // width)
    return max(at - reach, 0), min(at + reach + 1, blocks)


def dot_terms(left, right, left_dim, right_dim):
    return lax.dot_general(
        left, right, (((left_dim,), (right_dim,)), ((), ())), preferred_element_type=jnp.float32
    )


def load_heads(where_ref, packed_ref, cosine_ref, sine_ref, head_count, blocks, width):
    head = pl.program_id(0)
    half = HD // 2
    own = where_ref[3 * head_count]

    def rows_of(kind):
        start = pl.multiple_of(where_ref[kind * head_count + head] * HD, HD)
        pieces = []
        for block in range(blocks):
            at = pl.multiple_of(jnp.bitwise_xor(own, block) * width, width)
            pieces.append(packed_ref[pl.ds(start, HD), pl.ds(at, width)])
        return jnp.concatenate(pieces, axis=1)

    def turned(values):
        values = values.astype(jnp.float32)
        upper, lower = turn(values[:half], values[half:], cosine_ref[...], sine_ref[...])
        return jnp.concatenate([upper, lower], axis=0).astype(jnp.bfloat16)

    return turned(rows_of(0)), turned(rows_of(1)), rows_of(2)


def band_scores(queries, key_rows, at, first, last, width):
    factor = 1.0 / math.sqrt(HD)
    scores = factor * dot_terms(
        key_rows[:, first * width : last * width], queries[:, at * width : (at + 1) * width], 0, 0
    )
    key_at = first * width + lax.broadcasted_iota(jnp.int32, scores.shape, 0)
    query_at = at * width + lax.broadcasted_iota(jnp.int32, scores.shape, 1)
    in_band = jnp.abs(key_at - query_at) <= WINDOW // 2
    return jnp.where(in_band, scores, NEG)


def attend_kernel(
    head_count, blocks, where_ref, packed_ref, cosine_ref, sine_ref, mixture_ref, log_ref
):
    width = packed_ref.shape[1] // blocks
    head = pl.program_id(0)
    own = where_ref[3 * head_count]
    queries, key_rows, value_rows = load_heads(
        where_ref, packed_ref, cosine_ref, sine_ref, head_count, blocks, width
    )
    for at in range(blocks):
        first, last = key_span(at, blocks, width)
        scores = band_scores(queries, key_rows, at, first, last, width)
        row_max = jnp.max(scores, axis=0, keepdims=True)
        row_total = jnp.sum(jnp.exp(scores - row_max), axis=0, keepdims=True)
        log_total = row_max + jnp.log(row_total)
        weights = jnp.exp(scores - log_total).astype(jnp.bfloat16)
        mixture = dot_terms(value_rows[:, first * width : last * width], weights, 1, 0)
        to = pl.multiple_of(jnp.bitwise_xor(own, at) * width, width)
        mixture_ref[:, pl.ds(to, width)] = mixture.astype(jnp.bfloat16)
        log_ref[0, :, at * width : (at + 1) * width] = log_total


def attend_back_kernel(
    head_count,
    blocks,
    where_ref,
    packed_ref,
    cosine_ref,
    sine_ref,
    mixture_ref,
    log_ref,
    grad_ref,
    out_ref,
    query_sum,
    key_sum,
    value_sum,
):
    width = packed_ref.shape[1] // blocks
    half = HD // 2
    factor = 1.0 / math.sqrt(HD)
    head = pl.program_id(0)
    own = where_ref[3 * head_count]
    queries, key_rows, value_rows = load_heads(
        where_ref, packed_ref, cosine_ref, sine_ref, head_count, blocks, width
    )
    key_sum[...] = jnp.zeros_like(key_sum)
    value_sum[...] = jnp.zeros_like(value_sum)
    for at in range(blocks):
        first, last = key_span(at, blocks, width)
        low, high = first * width, last * width
        here = slice(at * width, (at + 1) * width)
        source = pl.multiple_of(jnp.bitwise_xor(own, at) * width, width)
        grad_mixture = grad_ref[:, pl.ds(source, width)]
        mixture = mixture_ref[:, pl.ds(source, width)]
        scores = band_scores(queries, key_rows, at, first, last, width)
        probability = jnp.exp(scores - log_ref[0, :, here])
        prob_low = probability.astype(jnp.bfloat16)
        value_sum[:, low:high] += dot_terms(grad_mixture, prob_low, 1, 1)
        grad_probs = dot_terms(value_rows[:, low:high], grad_mixture, 0, 0)
        delta_sum = jnp.sum(
            grad_mixture.astype(jnp.float32) * mixture.astype(jnp.float32), axis=0, keepdims=True
        )
        grad_scores = (probability * (grad_probs - delta_sum) * factor).astype(jnp.bfloat16)
        query_sum[:, here] = dot_terms(key_rows[:, low:high], grad_scores, 1, 0)
        key_sum[:, low:high] += dot_terms(queries[:, here], grad_scores, 1, 1)

    def put(kind, values):
        start = pl.multiple_of(where_ref[kind * head_count + head] * HD, HD)
        for block in range(blocks):
            to = pl.multiple_of(jnp.bitwise_xor(own, block) * width, width)
            out_ref[pl.ds(start, HD), pl.ds(to, width)] = values[
                :, block * width : (block + 1) * width
            ].astype(jnp.bfloat16)

    for kind, total in ((0, query_sum), (1, key_sum)):
        upper, lower = turn_back(total[:half], total[half:], cosine_ref[...], sine_ref[...])
        put(kind, jnp.concatenate([upper, lower], axis=0))
    put(2, value_sum[...])


def attention_specs(head_count, rows, length):
    whole = pl.BlockSpec((rows, length), lambda h, w: (0, 0))
    table = pl.BlockSpec((HD // 2, length), lambda h, w: (0, 0))
    head = pl.BlockSpec((HD, length), lambda h, w: (h, 0))
    logs = pl.BlockSpec((1, 1, length), lambda h, w: (h, 0, 0))
    return whole, table, head, logs


def attend_cost(head_count, length, products):
    return pl.CostEstimate(
        flops=2 * products * head_count * length * 3 * LANES * HD,
        bytes_accessed=8 * head_count * HD * length,
        transcendentals=2 * head_count * length * 3 * LANES,
    )


def attend(where, packed, cosine, sine, head_count, blocks):
    rows, length = packed.shape
    whole, table, head, logs = attention_specs(head_count, rows, length)

    def kernel(*refs):
        attend_kernel(head_count, blocks, *refs)

    return pl.pallas_call(
        kernel,
        out_shape=(
            jax.ShapeDtypeStruct((head_count * HD, length), jnp.bfloat16),
            jax.ShapeDtypeStruct((head_count, 1, length), jnp.float32),
        ),
        grid_spec=pltpu.PrefetchScalarGridSpec(
            num_scalar_prefetch=1,
            grid=(head_count,),
            in_specs=[whole, table, table],
            out_specs=[head, logs],
        ),
        cost_estimate=attend_cost(head_count, length, 2),
        name="attend",
    )(where, packed, cosine, sine)


def attend_back(where, packed, cosine, sine, mixture, logs_in, grad, head_count, blocks):
    rows, length = packed.shape
    whole, table, head, logs = attention_specs(head_count, rows, length)

    def kernel(*refs):
        attend_back_kernel(head_count, blocks, *refs)

    return pl.pallas_call(
        kernel,
        out_shape=jax.ShapeDtypeStruct((rows, length), jnp.bfloat16),
        grid_spec=pltpu.PrefetchScalarGridSpec(
            num_scalar_prefetch=1,
            grid=(head_count,),
            in_specs=[whole, table, table, head, logs, head],
            out_specs=whole,
            scratch_shapes=[pltpu.VMEM((HD, length), jnp.float32)] * 3,
        ),
        cost_estimate=attend_cost(head_count, length, 5),
        name="attend_back",
    )(where, packed, cosine, sine, mixture, logs_in, grad)


def row_norm(values):
    center = jnp.mean(values, axis=1, keepdims=True)
    spread = jnp.mean((values - center) ** 2, axis=1, keepdims=True)
    rescale = lax.rsqrt(spread + epsilon)
    return (values - center) * rescale, rescale


def row_norm_back(grads, normed, rescale, gain):
    scaled = grads * gain
    first_mean = jnp.mean(scaled, axis=1, keepdims=True)
    second_mean = jnp.mean(scaled * normed, axis=1, keepdims=True)
    return rescale * (scaled - first_mean - normed * second_mean)


def on_device_rings(
    block_input,
    attn_gain,
    qkv_weight,
    attn_weight,
    mlp_gain,
    inner_weight,
    outer_weight,
    output_grad,
):
    positions, sequences, quarter = block_input.shape
    gx_size, gy_size = lax.axis_size("gx"), lax.axis_size("gy")
    gx_at, gy_at = lax.axis_index("gx"), lax.axis_index("gy")
    z_at, y_at = gx_at // 2, gx_at % 2
    depth = gx_size // 2
    length = positions * gx_size
    rows = length // gy_size
    width = quarter * gy_size
    head_count = quarter // HD
    unit_count = outer_weight.shape[0]
    units = -(-unit_count // (gy_size * SUBLANES)) * SUBLANES
    padding = gy_size * units - unit_count
    far_y = y_at == 1
    odd_z = (z_at % 2) == 1

    def own_sequence(blocks):
        tokens = lax.all_to_all(blocks, "gx", split_axis=1, concat_axis=0, tiled=True)
        tokens = tokens.reshape(gy_size, rows, quarter)
        return jnp.stack(by_xor(tokens, gy_at))

    def all_features(parts):
        parts = [jnp.concatenate([parts[j, f ^ j] for f in range(4)], axis=0) for j in range(4)]
        return jnp.concatenate(by_xor(parts, gy_at), axis=1)

    turned = qkv_weight.T
    other = swap_y(turned)
    pair = jnp.concatenate(
        [jnp.where(far_y, other, turned), jnp.where(far_y, turned, other)], axis=0
    )
    per_device = pair.shape[0] // (gy_size * HD)
    pair = jnp.moveaxis(pair.reshape(per_device, gy_size, HD, quarter), 1, 0)
    tokens = own_sequence(block_input)
    pair = spread_gy(pair)
    chunk_rows = per_device * HD
    pair = jnp.concatenate([pair[k].reshape(chunk_rows, quarter) for k in range(4)], axis=1)
    across = swap_x(tokens)
    qkv_one = ring_up(after(pair, tokens))
    both = jnp.stack([tokens, across])
    beyond = swap_core(both)
    source = all_features(jnp.stack([both[0], beyond[0], both[1], beyond[1]]))

    columns = attn_weight.shape[1]
    inner_blocks = jnp.pad(inner_weight.T, ((0, padding), (0, 0)))
    inner_blocks = inner_blocks.reshape(gy_size, units, quarter)
    attn_blocks = attn_weight.reshape(head_count, HD, columns)
    outer_blocks = jnp.pad(outer_weight, ((0, padding), (0, 0)))
    outer_blocks = outer_blocks.reshape(gy_size, units, columns)
    parts = [inner_blocks[:, :, k : k + columns] for k in range(0, quarter, columns)]
    parts = jnp.concatenate([*parts, outer_blocks, attn_blocks], axis=1)
    parts = spread_gy(after(parts, across))
    inner_part = jnp.concatenate(
        [
            parts[k, at * units : (at + 1) * units]
            for k in range(4)
            for at in range(quarter // columns)
        ],
        axis=1,
    )
    outer_start = quarter // columns * units
    outer_part = parts[:, outer_start : outer_start + units]
    attn_part = parts[:, outer_start + units :].reshape(head_count * HD, columns)

    def relate(blocks):
        blocks = [[blocks[2 * p + e] for e in range(2)] for p in range(2)]
        blocks = [[jnp.where(far_y, b[1 - e], b[e]) for e in range(2)] for b in blocks]
        return [jnp.where(odd_z, blocks[1 - p][e], blocks[p][e]) for p in range(2) for e in range(2)]

    outer_part = jnp.stack(relate(outer_part))
    gains = gather_quarters(after(jnp.stack([attn_gain, mlp_gain]), across))
    gains = jnp.concatenate(by_xor(gains, gy_at), axis=1)
    first_gain, second_gain = gains[:1], gains[1:]

    attn_pair = jnp.concatenate([attn_part, swap_y(attn_part)], axis=1)
    inner_far = [swap_y(inner_part)]
    outer_far = [swap_y(after(outer_part, qkv_one))]
    qkv_two = ring_up(after(qkv_one, attn_pair))
    attn_one = ring_up(after(attn_pair, qkv_one))
    qkv_three = ring_up(after(qkv_two, attn_one))
    attn_two = ring_up(after(attn_one, qkv_two))
    inner_one = ring_up(after(inner_part, qkv_two))
    qkv_whole = jnp.concatenate([pair, qkv_one, qkv_two, qkv_three], axis=0)

    normed_attn, rescale_attn = row_norm(source.astype(jnp.float32))
    low_attn = (normed_attn * first_gain).astype(jnp.bfloat16)
    packed = dot_terms(qkv_whole, low_attn, 1, 1).astype(jnp.bfloat16)
    half = HD // 2
    frequency = rope_base ** (-(2.0 * jnp.arange(half, dtype=jnp.float32)) / HD)
    angles = frequency[:, None] * jnp.arange(length, dtype=jnp.float32)[None, :]
    cosine, sine = jnp.cos(angles), jnp.sin(angles)
    order = jnp.arange(3 * head_count, dtype=jnp.int32)
    place = lax.rem(z_at - order // per_device + depth, depth) * per_device + order % per_device
    where = jnp.concatenate([place, gy_at[None]]).astype(jnp.int32)

    attn_three = ring_up(after(attn_two, packed))
    inner_two = ring_up(after(inner_one, packed))
    inner_far.append(swap_y(after(inner_one, packed)))
    outer_one = ring_up(after(outer_part, packed))
    mixture, log_total = attend(where, packed, cosine, sine, head_count, gy_size)
    inner_three = ring_up(after(inner_two, mixture))
    inner_far.append(swap_y(after(inner_two, mixture)))
    attn_whole = jnp.concatenate([attn_pair, attn_one, attn_two, attn_three], axis=1)

    def row_chunks(partial_sum):
        return partial_sum.astype(jnp.bfloat16).reshape(gy_size, rows, width)

    def gather_rows(piece):
        return gather_quarters(piece).reshape(length, width)

    attended = row_chunks(dot_terms(mixture, attn_whole, 0, 0))
    gradient_tokens = own_sequence(after(output_grad, attended))
    attended = scatter_quarters(attended)
    residual = source[:rows].astype(jnp.float32) + to_absolute(attended, z_at, y_at)
    inner_far.append(swap_y(after(inner_three, residual)))
    outer_two = ring_up(after(outer_one, residual))
    outer_far.append(swap_y(after(outer_one, residual)))

    normed_mlp, rescale_mlp = row_norm(residual)
    low_mlp = gather_rows((normed_mlp * second_gain).astype(jnp.bfloat16))
    inner_near = [inner_part, inner_one, inner_two, inner_three]
    inner_whole = jnp.concatenate(
        [piece for pieces in zip(inner_near, inner_far, strict=True) for piece in pieces], axis=0
    )
    outer_three = ring_up(after(outer_two, low_mlp))
    outer_far.append(swap_y(after(outer_two, low_mlp)))
    upstream = all_features(gather_quarters(after(gradient_tokens, residual)))
    upstream_turned = to_relative(upstream, z_at, y_at)
    gate_up = dot_terms(inner_whole, low_mlp, 1, 1)
    unit_rows = gy_size * units
    in_first = lax.broadcasted_iota(jnp.int32, (unit_rows, 1), 0) < unit_rows // 2
    first_is_gate = z_at < depth // 2
    second_is_gate = lax.rem(z_at + depth - 1, depth) < depth // 2
    is_gate = jnp.where(in_first, first_is_gate, second_is_gate)
    gate_part = jnp.where(is_gate, gate_up[:unit_rows], gate_up[unit_rows:])
    up_part = jnp.where(is_gate, gate_up[unit_rows:], gate_up[:unit_rows])
    activated, derivative = gelu_parts(gate_part)
    hidden = (activated * up_part).astype(jnp.bfloat16)
    outer_far.append(swap_y(after(outer_three, hidden)))
    outer_near = [outer_part, outer_one, outer_two, outer_three]
    outer_whole = jnp.concatenate(
        [
            jnp.concatenate(
                [
                    pieces[d][2 * ((p + d) % 2) + (e ^ far)]
                    for d in range(depth)
                    for far, pieces in enumerate((outer_near, outer_far))
                ],
                axis=1,
            )
            for p in range(2)
            for e in range(2)
        ],
        axis=0,
    )
    grad_hidden = dot_terms(outer_whole, upstream_turned, 1, 1)
    grad_gate = (grad_hidden * up_part * derivative).astype(jnp.bfloat16)
    grad_up = (grad_hidden * activated).astype(jnp.bfloat16)
    grad_gate_up = jnp.concatenate(
        [jnp.where(is_gate, grad_gate, grad_up), jnp.where(is_gate, grad_up, grad_gate)], axis=0
    )

    grad_chunks = row_chunks(dot_terms(grad_gate_up, inner_whole, 0, 0))
    grad_low_mlp = scatter_quarters(grad_chunks)
    grad_residual = upstream[:rows].astype(jnp.float32) + row_norm_back(
        grad_low_mlp, normed_mlp, rescale_mlp, second_gain
    )
    mlp_gain_term = jnp.sum(grad_low_mlp * normed_mlp, axis=0, keepdims=True)
    branch = to_relative(grad_residual.astype(jnp.bfloat16), z_at, y_at)
    branch = gather_rows(branch)

    outer_term = dot_terms(hidden, after(upstream_turned, grad_chunks), 1, 0).astype(jnp.bfloat16)
    outer_term = outer_term.reshape(2, 2, units, depth, 2, columns)

    def outer_chunk(d, far):
        return jnp.concatenate(
            [outer_term[(p + d) % 2, e ^ far, :, d, far] for p in range(2) for e in range(2)],
            axis=0,
        )

    outer_arrived = swap_y(jnp.stack([outer_chunk(d, 1) for d in range(depth)]))
    inner_term = dot_terms(after(grad_gate_up, grad_chunks), low_mlp, 1, 0).astype(jnp.bfloat16)
    inner_term = inner_term.reshape(depth, 2, units, width)
    inner_arrived = swap_y(inner_term[:, 1])

    grad_mixture = dot_terms(attn_whole, branch, 1, 1).astype(jnp.bfloat16)
    outer_arrived = after(outer_arrived, grad_mixture)
    outer_chunks = [add_low(outer_chunk(d, 0), outer_arrived[d]) for d in range(depth)]
    grad_packed = attend_back(
        where, packed, cosine, sine, mixture, log_total, grad_mixture, head_count, gy_size
    )
    inner_arrived = after(inner_arrived, grad_packed)
    inner_chunks = [add_low(inner_term[d, 0], inner_arrived[d]) for d in range(depth)]
    low_chunks = row_chunks(dot_terms(grad_packed, qkv_whole, 0, 0))
    qkv_term = dot_terms(grad_packed, low_attn, 1, 0).astype(jnp.bfloat16)
    qkv_term = qkv_term.reshape(depth, chunk_rows, width)
    grad_low_attn = scatter_quarters(low_chunks)
    normed_rows, rescale_rows = normed_attn[:rows], rescale_attn[:rows]
    attn_gain_term = jnp.sum(grad_low_attn * normed_rows, axis=0, keepdims=True)
    grad_input = grad_residual + row_norm_back(grad_low_attn, normed_rows, rescale_rows, first_gain)

    qkv_sum = scatter_ring([qkv_term[d] for d in range(depth)])
    qkv_sum = jnp.moveaxis(qkv_sum.reshape(chunk_rows, gy_size, quarter), 1, 0)
    qkv_sum = spread_gy(qkv_sum).reshape(gy_size, per_device, HD, quarter)
    qkv_sum = jnp.moveaxis(qkv_sum, 0, 1).reshape(2, qkv_weight.shape[1], quarter)
    kept = jnp.where(far_y, qkv_sum[1], qkv_sum[0])
    sent = swap_y(jnp.where(far_y, qkv_sum[0], qkv_sum[1]))
    qkv_out = (kept.astype(jnp.float32) + sent.astype(jnp.float32)).T

    outer_sum = scatter_ring(
        outer_chunks, ((grad_packed,), (low_chunks,), (grad_low_attn,))
    )
    inner_sum = scatter_ring(inner_chunks, ((low_chunks,), (grad_low_attn,), ()))
    attn_term = dot_terms(mixture, branch, 1, 0).astype(jnp.bfloat16)
    attn_sum = scatter_ring(
        jnp.split(attn_term, depth, axis=1), ((grad_packed,), (low_chunks,), (grad_low_attn,))
    )
    attn_sum = add_low(attn_sum[:, :columns], swap_y(attn_sum[:, columns:]))

    outer_sum = outer_sum.reshape(gy_size, units, columns)
    outer_sum = jnp.stack(relate(outer_sum))
    inner_sum = [
        jnp.moveaxis(inner_sum.reshape(units, gy_size, quarter), 1, 0)[:, :, k : k + columns]
        for k in range(0, quarter, columns)
    ]
    attn_sum = attn_sum.reshape(head_count, HD, columns)
    parts = spread_gy(jnp.concatenate([*inner_sum, outer_sum, attn_sum], axis=1))
    inner_sum = jnp.concatenate(
        [parts[:, at * units : (at + 1) * units] for at in range(quarter // columns)], axis=2
    )
    inner_out = inner_sum.reshape(unit_rows, quarter)[:unit_count].T
    outer_out = parts[:, outer_start : outer_start + units]
    outer_out = outer_out.reshape(unit_rows, columns)[:unit_count]
    attn_out = parts[:, outer_start + units :].reshape(head_count * HD, columns)

    projected = row_chunks(dot_terms(after(hidden, branch), outer_whole, 0, 0))
    projected = scatter_quarters(projected)
    result = residual + to_absolute(projected, z_at, y_at)

    def to_placement(values, terms):
        rest = 2 * SUBLANES
        high = terms.astype(jnp.bfloat16)
        low = (terms - high.astype(jnp.float32)).astype(jnp.bfloat16)
        pieces = jnp.concatenate([high, low], axis=0)
        pieces = jnp.pad(pieces, ((0, rest - pieces.shape[0]), (0, 0)))
        parts = jnp.concatenate([values.astype(jnp.bfloat16), pieces], axis=0)
        parts = jnp.moveaxis(parts.reshape(rows + rest, gy_size, quarter), 1, 0)
        parts = spread_gy(parts)
        count = terms.shape[0]

        def total(blocks):
            blocks = jnp.sum(blocks[:, : 2 * count].astype(jnp.float32), axis=0)
            return blocks[:count] + blocks[count:]

        sums = total(parts[:, rows:])
        high = sums.astype(jnp.bfloat16)
        low = (sums - high.astype(jnp.float32)).astype(jnp.bfloat16)
        pieces = jnp.pad(jnp.concatenate([high, low], axis=0), ((0, rest - 2 * count), (0, 0)))
        pieces = jnp.broadcast_to(pieces[None], (gx_size, rest, quarter))
        tokens = parts[:, :rows].reshape(gx_size, positions, quarter)
        tokens = jnp.concatenate([tokens, pieces], axis=1)
        blocks = lax.all_to_all(tokens, "gx", split_axis=0, concat_axis=0, tiled=True)
        placed = jnp.moveaxis(blocks[:, :positions], 0, 1).astype(jnp.float32)
        return placed, total(blocks[:, positions:])

    def to_placement_only(values):
        parts = values.astype(jnp.bfloat16).reshape(rows, gy_size, quarter)
        tokens = spread_gy(jnp.moveaxis(parts, 1, 0)).reshape(gx_size, positions, quarter)
        blocks = lax.all_to_all(tokens, "gx", split_axis=0, concat_axis=0, tiled=True)
        return jnp.moveaxis(blocks, 0, 1).astype(jnp.float32)

    terms = jnp.concatenate([attn_gain_term, mlp_gain_term], axis=0)
    placed_grad, gain_sums = to_placement(grad_input, terms)
    return (
        to_placement_only(result),
        placed_grad,
        gain_sums[0],
        qkv_out,
        attn_out.astype(jnp.float32),
        gain_sums[1],
        inner_out.astype(jnp.float32),
        outer_out.astype(jnp.float32),
    )


def solution(mesh):
    def on_device(*args):
        if rings_fit(args, mesh.shape["gx"], mesh.shape["gy"]):
            return on_device_rings(*args)
        return on_device_general(*args)

    return jax.shard_map(
        on_device,
        mesh=mesh,
        in_specs=(
            P("gx", None, "gy"),
            P("gy"),
            P("gy", "gx"),
            P("gy", "gx"),
            P("gy"),
            P("gy", "gx"),
            P("gy", "gx"),
            P("gx", None, "gy"),
        ),
        out_specs=(
            P("gx", None, "gy"),
            P("gx", None, "gy"),
            P("gy"),
            P("gy", "gx"),
            P("gy", "gx"),
            P("gy"),
            P("gy", "gx"),
            P("gy", "gx"),
        ),
        check_vma=False,
    )
```
